32 devices in a mesh: var: 4 (over x, core), space: 8 (over z, y).
Axes of the slice: x: 2, y: 2, z: 4, core: 2. Of those that a mesh axis runs over, the one named last changes fastest.
Arguments:
- fields: bfloat16 [8, 1024, 32768], P('var', None, 'space'), may hold values from -6 to 6
- eigenfunctions: bfloat16 [8, 64, 32768], P('var', None, 'space'), may hold values from -0.03125 to 0.03125
- start: float32 [512, 128], replicated, may hold values from -6 to 6
- grid_count: int32 [8], replicated, may hold values from 16384 to 32768
Outputs:
- loadings: bfloat16 [8, 128, 32768], P('var', None, 'space')
- component_scores: float32 [1024, 128], replicated
- explained: float32 [8, 1024], P('var')
The draws below stay inside these ranges and needn't reach their ends.
Inputs may be any that keep to these rules, and one draw needn't show every extreme that they name: The grid of variable v is its points 0 to grid_count[v] - 1.
All inputs are finite; a program needn't handle non-finite values.
Results may differ from the reference program's by a relative error of at most 0.005.
Values sent between devices are 32-bit elements; how exact they have to be, the bound alone decides.
A program may use at most 64 MiB of HBM per device.

```python
import jax
import jax.numpy as jnp
from jax import lax

V = 8
M = 64
K = 128
SWEEPS = 2
NS = 1024
G = 32768
JD = 512


def with_ends(array, rng, low, high):
    shape = array.shape
    index_at = [jax.random.randint(jax.random.fold_in(rng, axis), (), 0, shape[axis]) for axis in range(len(shape))]
    array = array.at[tuple(index_at)].set(low)
    longest = shape.index(max(shape))
    index_at[longest] = (index_at[longest] + 1) % shape[longest]
    return array.at[tuple(index_at)].set(high)


def block_scale(rng, dims, pieces, low, top_value):
    level, own = 1.0, jax.random.fold_in(rng, 6)
    for dim, blocks in pieces:
        heights = jnp.exp(jax.random.uniform(jax.random.fold_in(own, dim), (blocks,), jnp.float32, low / len(pieces), top_value / len(pieces)))
        level = level * jnp.repeat(heights, dims[dim] // blocks).reshape([-1 if axis == dim else 1 for axis in range(len(dims))])
    return level


def gaussian(stream_key, dims, scale, most, split=(), kind=jnp.bfloat16):
    level = block_scale(stream_key, dims, split, -0.22, 0.18) if split else 1.0
    array = jax.random.normal(stream_key, dims, jnp.float32) * scale * level
    return jnp.minimum(jnp.maximum(array, -most), most).astype(kind)


def setup_inputs(seed: int = 0) -> dict:
    keys = jax.random.split(jax.random.key(seed), 5)
    return {
        "fields": gaussian(keys[0], (V, NS, G), 1.0, 6.0, ((0, 4), (2, 8))),
        "eigenfunctions": gaussian(keys[1], (V, M, G), G ** -0.5, 0.03125, ((0, 4), (2, 8))),
        "start": gaussian(keys[2], (JD, K), 1.0, 6.0, (), jnp.float32),
        "grid_count": with_ends(jax.random.randint(keys[3], (V,), G // 2, G + 1), jax.random.fold_in(keys[3], 1), G // 2, G).astype(jnp.int32),
    }


def orthogonalize(image):
    gram = jnp.dot(image.T.astype(jnp.float32), image.astype(jnp.float32), precision=lax.Precision.HIGHEST, preferred_element_type=jnp.float32)
    lower = jnp.linalg.cholesky(gram)
    return jax.scipy.linalg.solve_triangular(lower, image.T, lower=True).T

def reference(fields, eigenfunctions, start, grid_count):
    points = jnp.arange(G, dtype=jnp.int32)
    valid = points[None, :] < grid_count[:, None]
    masked = jnp.where(valid[:, None, :], eigenfunctions, jnp.zeros((), eigenfunctions.dtype))

    def project(pair):
        return jnp.dot(pair[0].astype(jnp.float32), pair[1].T.astype(jnp.float32), preferred_element_type=jnp.float32)
    scores = lax.map(project, (fields, masked))
    joint = jnp.transpose(scores, (1, 0, 2)).reshape(NS, V * M)
    centred = joint - jnp.mean(joint, axis=0, keepdims=True)
    cov = jnp.dot(centred.T.astype(jnp.float32), centred.astype(jnp.float32), precision=lax.Precision.HIGHEST, preferred_element_type=jnp.float32) / (NS - 1)
    basis = start
    for sweep in range(SWEEPS):
        image = jnp.dot(cov.astype(jnp.float32), basis.astype(jnp.float32), precision=lax.Precision.HIGHEST, preferred_element_type=jnp.float32)
        basis = orthogonalize(image)
    component_scores = jnp.dot(centred.astype(jnp.float32), basis.astype(jnp.float32), precision=lax.Precision.HIGHEST, preferred_element_type=jnp.float32)
    basis_low = basis.astype(jnp.bfloat16).reshape(V, M, K)
    scores_low = component_scores.astype(jnp.bfloat16)

    def rebuild(trio):
        values, funcs, coeffs = trio
        loading = jnp.dot(coeffs.T.astype(jnp.float32), funcs.astype(jnp.float32), preferred_element_type=jnp.float32).astype(jnp.bfloat16)
        rebuilt = jnp.dot(scores_low.astype(jnp.float32), loading.astype(jnp.float32), preferred_element_type=jnp.float32)
        wide = values.astype(jnp.float32)
        deviation = wide - jnp.mean(wide, axis=0, keepdims=True)
        gain = jnp.sum(2.0 * deviation * rebuilt - rebuilt * rebuilt, axis=1) / M
        return (loading, gain)
    loadings, explained = lax.map(rebuild, (fields, masked, basis_low))
    return (loadings, component_scores, explained)
```

```python
import functools

import jax
import jax.numpy as jnp
from jax import lax
from jax.experimental import pallas as pl
from jax.experimental.pallas import tpu as pltpu
from jax.sharding import PartitionSpec as P

M = 64
SWEEPS = 2
MESH = pl.DeviceIdType.MESH
F32 = jnp.float32
BF16 = jnp.bfloat16
HIGHEST = lax.Precision.HIGHEST


def dot(left, right, dims, precision=None):
    return lax.dot_general(left, right, (dims, ((), ())), precision=precision, preferred_element_type=F32)


NN = ((1,), (0,))
NT = ((1,), (1,))
TN = ((0,), (0,))


def split(x):
    high = x.astype(BF16)
    return high, (x - high.astype(F32)).astype(BF16)


def dot3(left, right, dims):
    (lh, ll), (rh, rl) = left, right
    return dot(lh, rh, dims) + (dot(lh, rl, dims) + dot(ll, rh, dims))


def remote(src, dst, send, recv, target):
    return pltpu.make_async_remote_copy(
        src_ref=src, dst_ref=dst, send_sem=send, recv_sem=recv, device_id=target, device_id_type=MESH
    )


def gather_kernel(
    n, nv, fields, masked, centred_ref, gram_ref,
    fbuf, part, rbuf, red, gpart, grbuf, gred, gfull, jbuf,
    fsem, asend, arecv, gsend, grecv, bsend, brecv, csend, crecv, dsend, drecv, hsend, hrecv,
):
    var, me = lax.axis_index("var"), lax.axis_index("space")
    local_vars, samples, _ = fields.shape
    rows = samples // n
    width = local_vars * M
    own_columns = pl.ds(pl.multiple_of(var * width, width), width)
    partner = var + 1 - 2 * (var % 2)
    half = rows // 2

    def at(i):
        return lax.rem(me + 1 + i, n)

    def fetch(i):
        block = pl.ds(pl.multiple_of(at(i) * rows, rows), rows)
        slot = lax.rem(i, 3)
        return pltpu.make_async_copy(fields.at[:, block, :], fbuf.at[slot], fsem.at[slot])

    fetch(0).start()
    fetch(1).start()

    barrier = pltpu.get_barrier_semaphore()
    for d in range(1, n):
        pl.semaphore_signal(barrier, inc=1, device_id=(var, lax.rem(me + d, n)), device_id_type=MESH)
    for d in range(1, nv):
        pl.semaphore_signal(barrier, inc=1, device_id=(lax.rem(var + d, nv), me), device_id_type=MESH)

    gram = jnp.concatenate([dot(masked[v], masked[v], NT) for v in range(local_vars)], axis=1)
    grows = M // n
    gpart[...] = jnp.zeros_like(gpart)
    for s in range(n):
        gpart[s, 0:grows, :] = gram[s * grows:(s + 1) * grows, :]

    pl.semaphore_wait(barrier, n - 1 + nv - 1)

    def send_part(i):
        return remote(part.at[i], rbuf.at[i], asend.at[i], arecv.at[i], (var, at(i)))

    def send_gram(i):
        return remote(gpart.at[at(i)], grbuf.at[i], gsend.at[i], grecv.at[i], (var, at(i)))

    def step(i, carry):
        slot = lax.rem(i, 3)

        @pl.when(i + 2 < n)
        def _():
            fetch(i + 2).start()

        @pl.when(i > 0)
        def _():
            send_part(i - 1).start()
            send_gram(i - 1).start()

        fetch(i).wait()
        part[i] = jnp.concatenate(
            [dot(fbuf[slot, v], masked[v], NT) for v in range(local_vars)], axis=1
        )
        return carry

    lax.fori_loop(0, n, step, 0)

    def wait_part(i, carry):
        send_part(i).wait()
        send_gram(i).wait()
        return carry

    lax.fori_loop(0, n - 1, wait_part, 0)

    total = part[n - 1]
    gtotal = gpart[me]
    for i in range(n - 1):
        total = total + rbuf[i]
        gtotal = gtotal + grbuf[i]
    red[...] = total
    gred[...] = gtotal
    own_rows = pl.ds(pl.multiple_of(me * rows, rows), rows)
    jbuf[own_rows, own_columns] = total
    gfull[me] = gtotal

    def send_columns(d):
        return remote(
            red, jbuf.at[own_rows, own_columns], bsend.at[d - 1], brecv.at[d - 1], (lax.rem(var + d, nv), me)
        )

    def send_gfull(d):
        return remote(gred, gfull.at[me], hsend.at[d - 1], hrecv.at[d - 1], (var, lax.rem(me + d, n)))

    for d in range(1, nv):
        send_columns(d).start()
    for d in range(1, nv):
        send_columns(d).wait()

    def half_block(s):
        return jbuf.at[pl.ds(pl.multiple_of(s * rows + lax.rem(var, 2) * half, half), half), :]

    def send_rows(d):
        return remote(half_block(me), half_block(me), csend.at[d - 1], crecv.at[d - 1], (var, lax.rem(me + d, n)))

    def pass_on(d):
        source = lax.rem(me - d + n, n)
        return remote(half_block(source), half_block(source), dsend.at[d - 1], drecv.at[d - 1], (partner, me))

    for d in range(1, n):
        send_rows(d).start()
    for d in range(1, n):
        send_gfull(d).start()
    for d in range(1, n):
        send_rows(d).wait_recv()
        pass_on(d).start()
    for d in range(1, n):
        send_gfull(d).wait()
        send_rows(d).wait_send()
    for d in range(1, n):
        pass_on(d).wait()

    mean = jnp.sum(jbuf[...], axis=0, keepdims=True) / samples
    centred_ref[...] = jbuf[...] - mean
    for s in range(n):
        gram_ref[s * grows:(s + 1) * grows, :] = gfull[s, 0:grows, :]


def gather_scores(n, nv, fields, masked):
    local_vars, samples, points = fields.shape
    rows = samples // n
    width = local_vars * M
    dma = pltpu.SemaphoreType.DMA
    return pl.pallas_call(
        functools.partial(gather_kernel, n, nv),
        out_shape=(
            jax.ShapeDtypeStruct((samples, nv * width), F32),
            jax.ShapeDtypeStruct((M, width), F32),
        ),
        in_specs=[pl.BlockSpec(memory_space=pl.ANY), pl.BlockSpec(memory_space=pltpu.VMEM)],
        out_specs=(pl.BlockSpec(memory_space=pltpu.VMEM), pl.BlockSpec(memory_space=pltpu.VMEM)),
        scratch_shapes=[
            pltpu.VMEM((3, local_vars, rows, points), BF16),
            pltpu.VMEM((n, rows, width), F32),
            pltpu.VMEM((n - 1, rows, width), F32),
            pltpu.VMEM((rows, width), F32),
            pltpu.VMEM((n, 8, width), F32),
            pltpu.VMEM((n - 1, 8, width), F32),
            pltpu.VMEM((8, width), F32),
            pltpu.VMEM((n, 8, width), F32),
            pltpu.VMEM((samples, nv * width), F32),
            dma((3,)),
            dma((n - 1,)), dma((n - 1,)),
            dma((n - 1,)), dma((n - 1,)),
            dma((nv - 1,)), dma((nv - 1,)),
            dma((n - 1,)), dma((n - 1,)),
            dma((n - 1,)), dma((n - 1,)),
            dma((n - 1,)), dma((n - 1,)),
        ],
        compiler_params=pltpu.CompilerParams(
            collective_id=0, has_side_effects=True, vmem_limit_bytes=48 * 1024 * 1024
        ),
        name="gather_scores",
    )(fields, masked)


def inverse_factor(gram):
    size = gram.shape[0]
    tiles = size // 8
    rows = [gram[8 * i:8 * i + 8, :] for i in range(tiles)]
    lane = lax.broadcasted_iota(jnp.int32, (1, size), 1)
    lane8 = lax.broadcasted_iota(jnp.int32, (8, size), 1)
    sublane = lax.broadcasted_iota(jnp.int32, (8, size), 0)
    done = []
    for k in range(size):
        tile, at = k // 8, k % 8
        columns = {i: jnp.broadcast_to(rows[i][:, k:k + 1], (8, size)) for i in range(tile, tiles)}
        pivot = columns[tile][at:at + 1, :]
        row = jnp.where(lane == k, 1.0, rows[tile][at:at + 1, :])
        done.append(jnp.where(lane <= k, row, 0.0) * lax.rsqrt(pivot))
        scaled = jnp.broadcast_to(row * (1.0 / pivot), (8, size))
        for i in range(tile, tiles):
            new = jnp.where(lane8 == k, 0.0, rows[i]) - columns[i] * scaled
            rows[i] = jnp.where(sublane > at, new, rows[i]) if i == tile else new
    return done


def basis_kernel(
    centred_ref, gram_ref, start_ref, masked_ref, loadings_ref, scores_ref, explained_ref,
    high_ref, low_ref, cov_high, cov_low, basis_ref, inverse_ref,
):
    var = lax.axis_index("var")
    samples = centred_ref.shape[0]
    local_vars = masked_ref.shape[0]
    width = local_vars * M
    high, low = split(centred_ref[...])
    high_ref[...] = high
    low_ref[...] = low
    cov = dot3((high, low), (high, low), TN) / (samples - 1)
    cov_high[...], cov_low[...] = split(cov)
    basis_ref[...] = start_ref[...]

    def sweep(_, carry):
        image = dot3((cov_high[...], cov_low[...]), split(basis_ref[...]), NN)
        gram = dot(image, image, TN, HIGHEST)
        for k, row in enumerate(inverse_factor(gram)):
            inverse_ref[k:k + 1, :] = row
        basis_ref[...] = dot(image, inverse_ref[...], NT, HIGHEST)
        return carry

    lax.fori_loop(0, SWEEPS, sweep, 0)

    scores = dot3((high_ref[...], low_ref[...]), split(basis_ref[...]), NN)
    scores_ref[...] = scores
    scores_low = scores.astype(BF16)
    own = pl.ds(pl.multiple_of(var * width, width), width)
    basis_low = basis_ref[own, :].astype(BF16)
    own_high, own_low = high_ref[:, own], low_ref[:, own]
    ones = jnp.ones((8, basis_low.shape[1]), F32)
    scores_wide = scores_low.astype(F32)
    for v in range(local_vars):
        mine = basis_low[v * M:(v + 1) * M, :]
        loadings_ref[v] = dot(mine, masked_ref[v], TN).astype(BF16)
        left, right = own_high[:, v * M:(v + 1) * M], own_low[:, v * M:(v + 1) * M]
        cross = dot(left, mine, NN) + dot(right, mine, NN)
        wide = mine.astype(F32)
        inner = dot(gram_ref[:, v * M:(v + 1) * M], wide, NN, HIGHEST)
        square = split(dot(wide, inner, TN, HIGHEST))
        quad = dot(scores_low, square[0], NN) + dot(scores_low, square[1], NN)
        gain = scores_wide * (2.0 * cross - quad)
        summed = dot(ones, gain, NT, HIGHEST) / M
        explained_ref[v:v + 1, :] = summed[0:1, :]


def finish(centred, gram, start, masked):
    local_vars, _, points = masked.shape
    samples, joint = centred.shape
    k = start.shape[1]
    return pl.pallas_call(
        basis_kernel,
        out_shape=(
            jax.ShapeDtypeStruct((local_vars, k, points), BF16),
            jax.ShapeDtypeStruct((samples, k), F32),
            jax.ShapeDtypeStruct((local_vars, samples), F32),
        ),
        in_specs=[pl.BlockSpec(memory_space=pltpu.VMEM)] * 4,
        out_specs=(pl.BlockSpec(memory_space=pltpu.VMEM),) * 3,
        scratch_shapes=[
            pltpu.VMEM((samples, joint), BF16),
            pltpu.VMEM((samples, joint), BF16),
            pltpu.VMEM((joint, joint), BF16),
            pltpu.VMEM((joint, joint), BF16),
            pltpu.VMEM((joint, k), F32),
            pltpu.VMEM((k, k), F32),
        ],
        compiler_params=pltpu.CompilerParams(vmem_limit_bytes=48 * 1024 * 1024),
        name="finish",
    )(centred, gram, start, masked)


def shards(n, nv, fields, eigenfunctions, start, grid_count):
    local_vars, samples, local_points = fields.shape
    first_var = lax.axis_index("var") * local_vars
    counts = lax.dynamic_slice_in_dim(grid_count, first_var, local_vars, 0)
    points = lax.axis_index("space") * local_points + jnp.arange(local_points, dtype=jnp.int32)
    valid = points[None, :] < counts[:, None]
    masked = jnp.where(valid[:, None, :], eigenfunctions, jnp.zeros((), eigenfunctions.dtype))
    centred, gram = gather_scores(n, nv, fields, masked)
    return finish(centred, gram, start, masked)


def solution(mesh):
    return jax.shard_map(
        functools.partial(shards, mesh.shape["space"], mesh.shape["var"]),
        mesh=mesh,
        in_specs=(P("var", None, "space"), P("var", None, "space"), P(), P()),
        out_specs=(P("var", None, "space"), P(), P("var", None)),
        check_vma=False,
    )
```

```python
import functools

import jax
import jax.numpy as jnp
from jax import lax
from jax.experimental import pallas as pl
from jax.experimental.pallas import tpu as pltpu
from jax.sharding import PartitionSpec as P

M = 64
SWEEPS = 2
MESH = pl.DeviceIdType.MESH
F32 = jnp.float32
BF16 = jnp.bfloat16
HIGHEST = lax.Precision.HIGHEST


def dot(left, right, dims, precision=None):
    return lax.dot_general(left, right, (dims, ((), ())), precision=precision, preferred_element_type=F32)


NN = ((1,), (0,))
NT = ((1,), (1,))
TN = ((0,), (0,))


def split(x):
    high = x.astype(BF16)
    return high, (x - high.astype(F32)).astype(BF16)


def dot3(left, right, dims):
    (lh, ll), (rh, rl) = left, right
    return dot(lh, rh, dims) + (dot(lh, rl, dims) + dot(ll, rh, dims))


def remote(src, dst, send, recv, target):
    return pltpu.make_async_remote_copy(
        src_ref=src, dst_ref=dst, send_sem=send, recv_sem=recv, device_id=target, device_id_type=MESH
    )


def masked_block(count, eigen, first):
    points = first + lax.broadcasted_iota(jnp.int32, (1, eigen.shape[1]), 1)
    return eigen * jnp.where(points < count, 1.0, 0.0).astype(eigen.dtype)


def gather_kernel(
    n, nv, counts, fields, eigen, centred_ref, gram_ref,
    fbuf, weights, part, rbuf, red, gpart, grbuf, gred, gfull, jbuf,
    fsem, asend, arecv, gsend, grecv, hsend, hrecv,
    zsend, zrecv, xsend, xrecv, ysend, yrecv, usend, urecv, wsend, wrecv, psend, precv,
):
    var, me = lax.axis_index("var"), lax.axis_index("space")
    local_vars, samples, local_points = fields.shape
    rows = samples // n
    width = local_vars * M
    half = rows // 2
    na, nz = nv // 2, n // 2
    side, core = var // 2, lax.rem(var, 2)
    depth, lane_y = me // 2, lax.rem(me, 2)
    partner = 2 * side + 1 - core

    def at(i):
        return 2 * lax.rem(depth + 1 + i // 2, nz) + lax.rem(lane_y + 1 + lax.rem(i, 2), 2)

    def fetch(i):
        block = pl.ds(pl.multiple_of(at(i) * rows, rows), rows)
        slot = lax.rem(i, 3)
        return pltpu.make_async_copy(fields.at[:, block, :], fbuf.at[slot], fsem.at[slot])

    fetch(0).start()
    fetch(1).start()

    barrier = pltpu.get_barrier_semaphore()
    for d in range(1, n):
        pl.semaphore_signal(barrier, inc=1, device_id=(var, lax.rem(me + d, n)), device_id_type=MESH)
    for d in range(1, nv):
        pl.semaphore_signal(barrier, inc=1, device_id=(lax.rem(var + d, nv), me), device_id_type=MESH)

    grams = []
    for v in range(local_vars):
        masked = masked_block(counts[var * local_vars + v], eigen[v], me * local_points)
        grams.append(dot(masked, masked, NT))
        weights[:, v * M:(v + 1) * M] = masked.T
    gram = jnp.concatenate(grams, axis=1)
    grows = M // n
    gpart[...] = jnp.zeros_like(gpart)
    for s in range(n):
        gpart[s, 0:grows, :] = gram[s * grows:(s + 1) * grows, :]

    pl.semaphore_wait(barrier, n - 1 + nv - 1)

    def send_part(i):
        return remote(part.at[i], rbuf.at[i], asend.at[i], arecv.at[i], (var, at(i)))

    def send_gram(i):
        return remote(gpart.at[at(i)], grbuf.at[i], gsend.at[i], grecv.at[i], (var, at(i)))

    owner = lax.broadcasted_iota(jnp.int32, (rows, width), 1) // M

    def step(i, carry):
        slot = lax.rem(i, 3)

        @pl.when(i + 2 < n)
        def _():
            fetch(i + 2).start()

        @pl.when(i > 0)
        def _():
            send_part(i - 1).start()
            send_gram(i - 1).start()

        fetch(i).wait()
        scores = dot(fbuf[slot, 0], weights[...], NN)
        for v in range(1, local_vars):
            scores = jnp.where(owner == v, dot(fbuf[slot, v], weights[...], NN), scores)
        part[i] = scores
        return carry

    lax.fori_loop(0, n, step, 0)

    def wait_part(i, carry):
        send_part(i).wait()
        send_gram(i).wait()
        return carry

    lax.fori_loop(0, n - 1, wait_part, 0)

    def block(a, z, y, low=0, size=rows):
        return jbuf.at[
            pl.ds(pl.multiple_of((2 * z + y) * rows + low, size), size),
            pl.ds(pl.multiple_of((2 * a + core) * width, width), width),
        ]

    total = part[n - 1]
    gtotal = gpart[me]
    for i in range(n - 1):
        total = total + rbuf[i]
        gtotal = gtotal + grbuf[i]
    red[...] = total
    gred[...] = gtotal
    block(side, depth, lane_y)[...] = total
    gfull[me] = gtotal

    def from_depth(t):
        return lax.rem(depth - t + nz, nz)

    def send_gfull(d):
        return remote(gred, gfull.at[me], hsend.at[d - 1], hrecv.at[d - 1], (var, lax.rem(me + d, n)))

    def send_z(t):
        target = (var, 2 * lax.rem(depth + t, nz) + lane_y)
        return remote(red, block(side, depth, lane_y), zsend.at[t - 1], zrecv.at[t - 1], target)

    def other(e):
        return lax.rem(side + e, na)

    def back(e):
        return lax.rem(side - e + na, na)

    beside = 1 - lane_y

    def send_x(t, e):
        mine = block(side, from_depth(t), lane_y)
        j = t * (na - 1) + e - 1
        return remote(red if t == 0 else mine, mine, xsend.at[j], xrecv.at[j], (2 * other(e) + core, me))

    def send_y(t):
        mine = block(side, from_depth(t), lane_y)
        return remote(red if t == 0 else mine, mine, ysend.at[t], yrecv.at[t], (var, 2 * depth + beside))

    def relay_y(t, e):
        piece = block(back(e), from_depth(t), lane_y, 0, half)
        j = t * (na - 1) + e - 1
        return remote(piece, piece, usend.at[j], urecv.at[j], (var, 2 * depth + beside))

    def relay_x(t, e):
        piece = block(side, from_depth(t), beside, half, half)
        j = t * (na - 1) + e - 1
        return remote(piece, piece, wsend.at[j], wrecv.at[j], (2 * other(e) + core, me))

    def to_partner(t, e, y):
        piece = block(back(e), from_depth(t), lane_y if y == 0 else beside)
        j = (t * na + e) * 2 + y
        return remote(piece, piece, psend.at[j], precv.at[j], (partner, me))

    for t in range(1, nz):
        send_z(t).start()
    for s in range(nz + 2):
        if s < nz:
            if s > 0:
                send_z(s).wait_recv()
            for e in range(1, na):
                send_x(s, e).start()
            send_y(s).start()
            to_partner(s, 0, 0).start()
            if s == 0:
                for d in range(1, n):
                    send_gfull(d).start()
        if 0 <= s - 1 < nz:
            for e in range(1, na):
                send_x(s - 1, e).wait_recv()
                relay_y(s - 1, e).start()
                to_partner(s - 1, e, 0).start()
            send_y(s - 1).wait_recv()
            for e in range(1, na):
                relay_x(s - 1, e).start()
            to_partner(s - 1, 0, 1).start()
        if 0 <= s - 2 < nz:
            for e in range(1, na):
                relay_y(s - 2, e).wait_recv()
                relay_x(s - 2, e).wait_recv()
                to_partner(s - 2, e, 1).start()
    for d in range(1, n):
        send_gfull(d).wait()
    for t in range(1, nz):
        send_z(t).wait_send()
    for t in range(nz):
        send_y(t).wait_send()
        for e in range(1, na):
            send_x(t, e).wait_send()
            relay_y(t, e).wait_send()
            relay_x(t, e).wait_send()
        for e in range(na):
            for y in range(2):
                to_partner(t, e, y).wait()

    mean = jnp.sum(jbuf[...], axis=0, keepdims=True) / samples
    centred_ref[...] = jbuf[...] - mean
    for s in range(n):
        gram_ref[s * grows:(s + 1) * grows, :] = gfull[s, 0:grows, :]


def gather_scores(n, nv, counts, fields, eigen):
    local_vars, samples, points = fields.shape
    rows = samples // n
    width = local_vars * M
    na, nz = nv // 2, n // 2
    dma = pltpu.SemaphoreType.DMA
    pairs = [n - 1, n - 1, n - 1, nz - 1, nz * (na - 1), nz, nz * (na - 1), nz * (na - 1), 2 * nz * na]
    return pl.pallas_call(
        functools.partial(gather_kernel, n, nv),
        out_shape=(
            jax.ShapeDtypeStruct((samples, nv * width), F32),
            jax.ShapeDtypeStruct((M, width), F32),
        ),
        in_specs=[
            pl.BlockSpec(memory_space=pltpu.SMEM),
            pl.BlockSpec(memory_space=pl.ANY),
            pl.BlockSpec(memory_space=pltpu.VMEM),
        ],
        out_specs=(pl.BlockSpec(memory_space=pltpu.VMEM), pl.BlockSpec(memory_space=pltpu.VMEM)),
        scratch_shapes=[
            pltpu.VMEM((3, local_vars, rows, points), BF16),
            pltpu.VMEM((points, width), BF16),
            pltpu.VMEM((n, rows, width), F32),
            pltpu.VMEM((n - 1, rows, width), F32),
            pltpu.VMEM((rows, width), F32),
            pltpu.VMEM((n, 8, width), F32),
            pltpu.VMEM((n - 1, 8, width), F32),
            pltpu.VMEM((8, width), F32),
            pltpu.VMEM((n, 8, width), F32),
            pltpu.VMEM((samples, nv * width), F32),
            dma((3,)),
            *[dma((count,)) for count in pairs for _ in range(2)],
        ],
        compiler_params=pltpu.CompilerParams(
            collective_id=0, has_side_effects=True, vmem_limit_bytes=48 * 1024 * 1024
        ),
        name="gather_scores",
    )(counts, fields, eigen)


def inverse_factor(gram):
    size = gram.shape[0]
    tiles = size // 8
    rows = [gram[8 * i:8 * i + 8, :] for i in range(tiles)]
    lane = lax.broadcasted_iota(jnp.int32, (8, size), 1)
    sublane = lax.broadcasted_iota(jnp.int32, (8, size), 0)

    def column(tile, k):
        return jnp.broadcast_to(tile[:, k:k + 1], (8, size))

    def spread(tile, j):
        return jnp.broadcast_to(tile[j:j + 1, :], (8, size))

    done = []
    for b in range(tiles):
        base = 8 * b
        inside = (lane >= base) & (lane < base + 8)
        tops = [column(rows[b], base + j) for j in range(8)]
        entry = {(i, j): spread(tops[j], i) for j in range(8) for i in range(j, 8)}
        unit = jnp.where(inside, jnp.where(lane - base == sublane, 1.0, 0.0), rows[b])
        line = [spread(unit, j) for j in range(8)]
        inverse = []
        for j in range(8):
            inverse.append(1.0 / entry[j, j])
            for i in range(j + 1, 8):
                factor = entry[i, j] * inverse[j]
                for q in range(j + 1, i + 1):
                    entry[i, q] = entry[i, q] - factor * entry[q, j]
                line[i] = line[i] - factor * line[j]
        rest = line[0]
        pivot = entry[0, 0]
        for j in range(1, 8):
            rest = jnp.where(sublane == j, line[j], rest)
            pivot = jnp.where(sublane == j, entry[j, j], pivot)
        done.append(jnp.where(lane < base + 8, rest, 0.0) * lax.rsqrt(pivot))
        for i in range(b + 1, tiles):
            new = jnp.where(inside, 0.0, rows[i])
            factors = []
            for j in range(8):
                value = column(rows[i], base + j)
                for p in range(j):
                    value = value - factors[p] * entry[j, p]
                factors.append(value * inverse[j])
            for j in range(8):
                new = new - factors[j] * line[j]
            rows[i] = new
    return done


def basis_kernel(
    counts, centred_ref, gram_ref, start_ref, eigen_ref, loadings_ref, scores_ref, explained_ref,
    high_ref, low_ref, cov_high, cov_low, basis_ref, inverse_ref,
):
    var = lax.axis_index("var")
    samples = centred_ref.shape[0]
    local_vars = eigen_ref.shape[0]
    first_point = lax.axis_index("space") * eigen_ref.shape[2]
    width = local_vars * M
    high, low = split(centred_ref[...])
    high_ref[...] = high
    low_ref[...] = low
    cov = dot3((high, low), (high, low), TN) / (samples - 1)
    cov_high[...], cov_low[...] = split(cov)
    basis_ref[...] = start_ref[...]

    def sweep(_, carry):
        image = dot3((cov_high[...], cov_low[...]), split(basis_ref[...]), NN)
        gram = dot(image, image, TN, HIGHEST)
        for i, tile in enumerate(inverse_factor(gram)):
            inverse_ref[8 * i:8 * i + 8, :] = tile
        basis_ref[...] = dot(image, inverse_ref[...], NT, HIGHEST)
        return carry

    lax.fori_loop(0, SWEEPS, sweep, 0)

    scores = dot3((high_ref[...], low_ref[...]), split(basis_ref[...]), NN)
    scores_ref[...] = scores
    scores_low = scores.astype(BF16)
    own = pl.ds(pl.multiple_of(var * width, width), width)
    basis_low = basis_ref[own, :].astype(BF16)
    own_high, own_low = high_ref[:, own], low_ref[:, own]
    ones = jnp.ones((8, basis_low.shape[1]), F32)
    scores_wide = scores_low.astype(F32)
    for v in range(local_vars):
        mine = basis_low[v * M:(v + 1) * M, :]
        masked = masked_block(counts[var * local_vars + v], eigen_ref[v], first_point)
        loadings_ref[v] = dot(mine, masked, TN).astype(BF16)
        left, right = own_high[:, v * M:(v + 1) * M], own_low[:, v * M:(v + 1) * M]
        cross = dot(left, mine, NN) + dot(right, mine, NN)
        wide = mine.astype(F32)
        inner = dot(gram_ref[:, v * M:(v + 1) * M], wide, NN, HIGHEST)
        square = split(dot(wide, inner, TN, HIGHEST))
        quad = dot(scores_low, square[0], NN) + dot(scores_low, square[1], NN)
        gain = scores_wide * (2.0 * cross - quad)
        summed = dot(ones, gain, NT, HIGHEST) / M
        explained_ref[v:v + 1, :] = summed[0:1, :]


def finish(counts, centred, gram, start, eigen):
    local_vars, _, points = eigen.shape
    samples, joint = centred.shape
    k = start.shape[1]
    return pl.pallas_call(
        basis_kernel,
        out_shape=(
            jax.ShapeDtypeStruct((local_vars, k, points), BF16),
            jax.ShapeDtypeStruct((samples, k), F32),
            jax.ShapeDtypeStruct((local_vars, samples), F32),
        ),
        in_specs=[pl.BlockSpec(memory_space=pltpu.SMEM)] + [pl.BlockSpec(memory_space=pltpu.VMEM)] * 4,
        out_specs=(pl.BlockSpec(memory_space=pltpu.VMEM),) * 3,
        scratch_shapes=[
            pltpu.VMEM((samples, joint), BF16),
            pltpu.VMEM((samples, joint), BF16),
            pltpu.VMEM((joint, joint), BF16),
            pltpu.VMEM((joint, joint), BF16),
            pltpu.VMEM((joint, k), F32),
            pltpu.VMEM((k, k), F32),
        ],
        compiler_params=pltpu.CompilerParams(vmem_limit_bytes=48 * 1024 * 1024),
        name="finish",
    )(counts, centred, gram, start, eigen)


def shards(n, nv, fields, eigenfunctions, start, grid_count):
    centred, gram = gather_scores(n, nv, grid_count, fields, eigenfunctions)
    return finish(grid_count, centred, gram, start, eigenfunctions)


def solution(mesh):
    return jax.shard_map(
        functools.partial(shards, mesh.shape["space"], mesh.shape["var"]),
        mesh=mesh,
        in_specs=(P("var", None, "space"), P("var", None, "space"), P(), P()),
        out_specs=(P("var", None, "space"), P(), P("var", None)),
        check_vma=False,
    )
```

```python
import functools

import jax
import jax.numpy as jnp
from jax import lax
from jax.experimental import pallas as pl
from jax.experimental.pallas import tpu as pltpu
from jax.sharding import PartitionSpec as P

M = 64
SWEEPS = 2
MESH = pl.DeviceIdType.MESH
F32 = jnp.float32
BF16 = jnp.bfloat16
HIGHEST = lax.Precision.HIGHEST


def dot(left, right, dims, precision=None):
    return lax.dot_general(left, right, (dims, ((), ())), precision=precision, preferred_element_type=F32)


NN = ((1,), (0,))
NT = ((1,), (1,))
TN = ((0,), (0,))


def split(x):
    high = x.astype(BF16)
    return high, (x - high.astype(F32)).astype(BF16)


def dot3(left, right, dims):
    (lh, ll), (rh, rl) = left, right
    return dot(lh, rh, dims) + (dot(lh, rl, dims) + dot(ll, rh, dims))


def remote(src, dst, send, recv, target):
    return pltpu.make_async_remote_copy(
        src_ref=src, dst_ref=dst, send_sem=send, recv_sem=recv, device_id=target, device_id_type=MESH
    )


def masked_block(count, eigen, first):
    points = first + lax.broadcasted_iota(jnp.int32, (1, eigen.shape[1]), 1)
    return eigen * jnp.where(points < count, 1.0, 0.0).astype(eigen.dtype)


def gather_kernel(
    n, nv, counts, fields, eigen_far, centred_ref, gram_ref,
    eigen, esem, fbuf, weights, part, rbuf, red, gpart, grbuf, gred, gfull, jbuf,
    fsem, asend, arecv, gsend, grecv, hsend, hrecv,
    zsend, zrecv, xsend, xrecv, ysend, yrecv, usend, urecv, wsend, wrecv, psend, precv,
):
    var, me = lax.axis_index("var"), lax.axis_index("space")
    local_vars, samples, local_points = fields.shape
    rows = samples // n
    width = local_vars * M
    half = rows // 2
    na, nz = nv // 2, n // 2
    side, core = var // 2, lax.rem(var, 2)
    depth, lane_y = me // 2, lax.rem(me, 2)
    partner = 2 * side + 1 - core

    def at(i):
        return 2 * lax.rem(depth + 1 + i // 2, nz) + lax.rem(lane_y + 1 + lax.rem(i, 2), 2)

    def fetch(i):
        block = pl.ds(pl.multiple_of(at(i) * rows, rows), rows)
        return pltpu.make_async_copy(fields.at[:, block, :], fbuf.at[i], fsem.at[i])

    eigen_copy = pltpu.make_async_copy(eigen_far, eigen, esem)
    eigen_copy.start()
    for i in range(n):
        fetch(i).start()

    barrier = pltpu.get_barrier_semaphore()
    for d in range(1, n):
        pl.semaphore_signal(barrier, inc=1, device_id=(var, lax.rem(me + d, n)), device_id_type=MESH)
    for d in range(1, nv):
        pl.semaphore_signal(barrier, inc=1, device_id=(lax.rem(var + d, nv), me), device_id_type=MESH)

    eigen_copy.wait()
    grams = []
    for v in range(local_vars):
        masked = masked_block(counts[var * local_vars + v], eigen[v], me * local_points)
        grams.append(dot(masked, masked, NT))
        weights[:, v * M:(v + 1) * M] = masked.T
    gram = jnp.concatenate(grams, axis=1)
    grows = M // n
    gpart[...] = jnp.zeros_like(gpart)
    for s in range(n):
        gpart[s, 0:grows, :] = gram[s * grows:(s + 1) * grows, :]

    pl.semaphore_wait(barrier, n - 1 + nv - 1)

    def send_part(i):
        return remote(part.at[i], rbuf.at[i], asend.at[i], arecv.at[i], (var, at(i)))

    def send_gram(i):
        return remote(gpart.at[at(i)], grbuf.at[i], gsend.at[i], grecv.at[i], (var, at(i)))

    owner = lax.broadcasted_iota(jnp.int32, (rows, width), 1) // M

    def step(i, carry):
        @pl.when(i > 0)
        def _():
            send_part(i - 1).start()
            send_gram(i - 1).start()

        fetch(i).wait()
        scores = dot(fbuf[i, 0], weights[...], NN)
        for v in range(1, local_vars):
            scores = jnp.where(owner == v, dot(fbuf[i, v], weights[...], NN), scores)
        part[i] = scores
        return carry

    lax.fori_loop(0, n, step, 0)

    def wait_part(i, carry):
        send_part(i).wait()
        send_gram(i).wait()
        return carry

    lax.fori_loop(0, n - 1, wait_part, 0)

    def block(a, z, y, low=0, size=rows):
        return jbuf.at[
            pl.ds(pl.multiple_of((2 * z + y) * rows + low, size), size),
            pl.ds(pl.multiple_of((2 * a + core) * width, width), width),
        ]

    total = part[n - 1]
    gtotal = gpart[me]
    for i in range(n - 1):
        total = total + rbuf[i]
        gtotal = gtotal + grbuf[i]
    red[...] = total
    gred[...] = gtotal
    block(side, depth, lane_y)[...] = total
    gfull[me] = gtotal

    def from_depth(t):
        return lax.rem(depth - t + nz, nz)

    def send_gfull(d):
        return remote(gred, gfull.at[me], hsend.at[d - 1], hrecv.at[d - 1], (var, lax.rem(me + d, n)))

    def send_z(t):
        target = (var, 2 * lax.rem(depth + t, nz) + lane_y)
        return remote(red, block(side, depth, lane_y), zsend.at[t - 1], zrecv.at[t - 1], target)

    def other(e):
        return lax.rem(side + e, na)

    def back(e):
        return lax.rem(side - e + na, na)

    beside = 1 - lane_y

    def send_x(t, e):
        mine = block(side, from_depth(t), lane_y)
        j = t * (na - 1) + e - 1
        return remote(red if t == 0 else mine, mine, xsend.at[j], xrecv.at[j], (2 * other(e) + core, me))

    def send_y(t):
        mine = block(side, from_depth(t), lane_y)
        return remote(red if t == 0 else mine, mine, ysend.at[t], yrecv.at[t], (var, 2 * depth + beside))

    def relay_y(t, e):
        piece = block(back(e), from_depth(t), lane_y, 0, half)
        j = t * (na - 1) + e - 1
        return remote(piece, piece, usend.at[j], urecv.at[j], (var, 2 * depth + beside))

    def relay_x(t, e):
        piece = block(side, from_depth(t), beside, half, half)
        j = t * (na - 1) + e - 1
        return remote(piece, piece, wsend.at[j], wrecv.at[j], (2 * other(e) + core, me))

    def to_partner(t, e, y):
        piece = block(back(e), from_depth(t), lane_y if y == 0 else beside)
        j = (t * na + e) * 2 + y
        return remote(piece, piece, psend.at[j], precv.at[j], (partner, me))

    for t in range(1, nz):
        send_z(t).start()
    for s in range(nz + 2):
        if s < nz:
            if s > 0:
                send_z(s).wait_recv()
            for e in range(1, na):
                send_x(s, e).start()
            send_y(s).start()
            to_partner(s, 0, 0).start()
            if s == 0:
                for d in range(1, n):
                    send_gfull(d).start()
        if 0 <= s - 1 < nz:
            for e in range(1, na):
                send_x(s - 1, e).wait_recv()
                relay_y(s - 1, e).start()
                to_partner(s - 1, e, 0).start()
            send_y(s - 1).wait_recv()
            for e in range(1, na):
                relay_x(s - 1, e).start()
            to_partner(s - 1, 0, 1).start()
        if 0 <= s - 2 < nz:
            for e in range(1, na):
                relay_y(s - 2, e).wait_recv()
                relay_x(s - 2, e).wait_recv()
                to_partner(s - 2, e, 1).start()
    for d in range(1, n):
        send_gfull(d).wait()
    for t in range(1, nz):
        send_z(t).wait_send()
    for t in range(nz):
        send_y(t).wait_send()
        for e in range(1, na):
            send_x(t, e).wait_send()
            relay_y(t, e).wait_send()
            relay_x(t, e).wait_send()
        for e in range(na):
            for y in range(2):
                to_partner(t, e, y).wait()

    mean = jnp.sum(jbuf[...], axis=0, keepdims=True) / samples
    centred_ref[...] = jbuf[...] - mean
    for s in range(n):
        gram_ref[s * grows:(s + 1) * grows, :] = gfull[s, 0:grows, :]


def gather_scores(n, nv, counts, fields, eigen):
    local_vars, samples, points = fields.shape
    rows = samples // n
    width = local_vars * M
    na, nz = nv // 2, n // 2
    dma = pltpu.SemaphoreType.DMA
    pairs = [n - 1, n - 1, n - 1, nz - 1, nz * (na - 1), nz, nz * (na - 1), nz * (na - 1), 2 * nz * na]
    return pl.pallas_call(
        functools.partial(gather_kernel, n, nv),
        out_shape=(
            jax.ShapeDtypeStruct((samples, nv * width), F32),
            jax.ShapeDtypeStruct((M, width), F32),
        ),
        in_specs=[
            pl.BlockSpec(memory_space=pltpu.SMEM),
            pl.BlockSpec(memory_space=pltpu.HBM),
            pl.BlockSpec(memory_space=pltpu.HBM),
        ],
        out_specs=(pl.BlockSpec(memory_space=pltpu.VMEM), pl.BlockSpec(memory_space=pltpu.VMEM)),
        scratch_shapes=[
            pltpu.VMEM((local_vars, M, points), BF16),
            dma,
            pltpu.VMEM((n, local_vars, rows, points), BF16),
            pltpu.VMEM((points, width), BF16),
            pltpu.VMEM((n, rows, width), F32),
            pltpu.VMEM((n - 1, rows, width), F32),
            pltpu.VMEM((rows, width), F32),
            pltpu.VMEM((n, 8, width), F32),
            pltpu.VMEM((n - 1, 8, width), F32),
            pltpu.VMEM((8, width), F32),
            pltpu.VMEM((n, 8, width), F32),
            pltpu.VMEM((samples, nv * width), F32),
            dma((n,)),
            *[dma((count,)) for count in pairs for _ in range(2)],
        ],
        compiler_params=pltpu.CompilerParams(
            collective_id=0, has_side_effects=True, vmem_limit_bytes=61 * 1024 * 1024
        ),
        name="gather_scores",
    )(counts, fields, eigen)


def inverse_factor(gram):
    size = gram.shape[0]
    tiles = size // 8
    rows = [gram[8 * i:8 * i + 8, :] for i in range(tiles)]
    lane = lax.broadcasted_iota(jnp.int32, (8, size), 1)
    sublane = lax.broadcasted_iota(jnp.int32, (8, size), 0)

    def column(tile, k):
        return jnp.broadcast_to(tile[:, k:k + 1], (8, size))

    def spread(tile, j):
        return jnp.broadcast_to(tile[j:j + 1, :], (8, size))

    done = []
    for b in range(tiles):
        base = 8 * b
        inside = (lane >= base) & (lane < base + 8)
        tops = [column(rows[b], base + j) for j in range(8)]
        entry = {(i, j): spread(tops[j], i) for j in range(8) for i in range(j, 8)}
        unit = jnp.where(inside, jnp.where(lane - base == sublane, 1.0, 0.0), rows[b])
        line = [spread(unit, j) for j in range(8)]
        inverse = []
        for j in range(8):
            inverse.append(1.0 / entry[j, j])
            for i in range(j + 1, 8):
                factor = entry[i, j] * inverse[j]
                for q in range(j + 1, i + 1):
                    entry[i, q] = entry[i, q] - factor * entry[q, j]
                line[i] = line[i] - factor * line[j]
        rest = line[0]
        pivot = entry[0, 0]
        for j in range(1, 8):
            rest = jnp.where(sublane == j, line[j], rest)
            pivot = jnp.where(sublane == j, entry[j, j], pivot)
        done.append(jnp.where(lane < base + 8, rest, 0.0) * lax.rsqrt(pivot))
        for i in range(b + 1, tiles):
            new = jnp.where(inside, 0.0, rows[i])
            factors = []
            for j in range(8):
                value = column(rows[i], base + j)
                for p in range(j):
                    value = value - factors[p] * entry[j, p]
                factors.append(value * inverse[j])
            for j in range(8):
                new = new - factors[j] * line[j]
            rows[i] = new
    return done


def basis_kernel(
    counts, centred_ref, gram_ref, start_far, eigen_far, loadings_ref, scores_ref, explained_ref,
    high_ref, low_ref, cov_high, cov_low, basis_ref, inverse_ref, eigen_ref, start_sem, eigen_sem,
):
    start_copy = pltpu.make_async_copy(start_far, basis_ref, start_sem)
    eigen_copy = pltpu.make_async_copy(eigen_far, eigen_ref, eigen_sem)
    start_copy.start()
    eigen_copy.start()
    var = lax.axis_index("var")
    samples = centred_ref.shape[0]
    local_vars = eigen_ref.shape[0]
    first_point = lax.axis_index("space") * eigen_ref.shape[2]
    width = local_vars * M
    high, low = split(centred_ref[...])
    high_ref[...] = high
    low_ref[...] = low
    cov = dot3((high, low), (high, low), TN) / (samples - 1)
    cov_high[...], cov_low[...] = split(cov)
    start_copy.wait()

    def sweep(_, carry):
        image = dot3((cov_high[...], cov_low[...]), split(basis_ref[...]), NN)
        gram = dot(image, image, TN, HIGHEST)
        for i, tile in enumerate(inverse_factor(gram)):
            inverse_ref[8 * i:8 * i + 8, :] = tile
        basis_ref[...] = dot(image, inverse_ref[...], NT, HIGHEST)
        return carry

    lax.fori_loop(0, SWEEPS, sweep, 0)

    scores = dot3((high_ref[...], low_ref[...]), split(basis_ref[...]), NN)
    scores_ref[...] = scores
    scores_low = scores.astype(BF16)
    own = pl.ds(pl.multiple_of(var * width, width), width)
    basis_low = basis_ref[own, :].astype(BF16)
    own_high, own_low = high_ref[:, own], low_ref[:, own]
    eigen_copy.wait()
    ones = jnp.ones((8, basis_low.shape[1]), F32)
    scores_wide = scores_low.astype(F32)
    for v in range(local_vars):
        mine = basis_low[v * M:(v + 1) * M, :]
        masked = masked_block(counts[var * local_vars + v], eigen_ref[v], first_point)
        loadings_ref[v] = dot(mine, masked, TN).astype(BF16)
        left, right = own_high[:, v * M:(v + 1) * M], own_low[:, v * M:(v + 1) * M]
        cross = dot(left, mine, NN) + dot(right, mine, NN)
        wide = mine.astype(F32)
        inner = dot(gram_ref[:, v * M:(v + 1) * M], wide, NN, HIGHEST)
        square = split(dot(wide, inner, TN, HIGHEST))
        quad = dot(scores_low, square[0], NN) + dot(scores_low, square[1], NN)
        gain = scores_wide * (2.0 * cross - quad)
        summed = dot(ones, gain, NT, HIGHEST) / M
        explained_ref[v:v + 1, :] = summed[0:1, :]


def finish(counts, centred, gram, start, eigen):
    local_vars, _, points = eigen.shape
    samples, joint = centred.shape
    k = start.shape[1]
    return pl.pallas_call(
        basis_kernel,
        out_shape=(
            jax.ShapeDtypeStruct((local_vars, k, points), BF16),
            jax.ShapeDtypeStruct((samples, k), F32),
            jax.ShapeDtypeStruct((local_vars, samples), F32),
        ),
        in_specs=[pl.BlockSpec(memory_space=pltpu.SMEM)]
        + [pl.BlockSpec(memory_space=pltpu.VMEM)] * 2
        + [pl.BlockSpec(memory_space=pltpu.HBM)] * 2,
        out_specs=(pl.BlockSpec(memory_space=pltpu.VMEM),) * 3,
        scratch_shapes=[
            pltpu.VMEM((samples, joint), BF16),
            pltpu.VMEM((samples, joint), BF16),
            pltpu.VMEM((joint, joint), BF16),
            pltpu.VMEM((joint, joint), BF16),
            pltpu.VMEM((joint, k), F32),
            pltpu.VMEM((k, k), F32),
            pltpu.VMEM((local_vars, M, points), BF16),
            pltpu.SemaphoreType.DMA,
            pltpu.SemaphoreType.DMA,
        ],
        compiler_params=pltpu.CompilerParams(vmem_limit_bytes=61 * 1024 * 1024),
        name="finish",
    )(counts, centred, gram, start, eigen)


def shards(n, nv, fields, eigenfunctions, start, grid_count):
    centred, gram = gather_scores(n, nv, grid_count, fields, eigenfunctions)
    return finish(grid_count, centred, gram, start, eigenfunctions)


def solution(mesh):
    return jax.shard_map(
        functools.partial(shards, mesh.shape["space"], mesh.shape["var"]),
        mesh=mesh,
        in_specs=(P("var", None, "space"), P("var", None, "space"), P(), P()),
        out_specs=(P("var", None, "space"), P(), P("var", None)),
        check_vma=False,
    )
```
